32 devices in a mesh: dp: 16 (over z, x, core), tensor: 2 (over y).
Axes of the slice: x: 2, y: 2, z: 4, core: 2. Of those that a mesh axis runs over, the one named last changes fastest.
Arguments:
- inputs: float32 [16, 256, 768], P('dp'), may hold values from -6 to 6
- condition: float32 [16, 768], P('dp'), may hold values from -2.5 to 2.5
- cotangent: float32 [16, 256, 768], P('dp'), may hold values from -6 to 6
- w_qkv: float32 [2, 768, 3, 768], P(None, None, None, 'tensor'), may hold values from -0.21875 to 0.21875
- b_qv: float32 [2, 2, 768], P(None, None, 'tensor'), may hold values from -1.25 to 1.25
- w_out: float32 [2, 768, 768], P(None, 'tensor'), may hold values from -0.875 to 0.875
- b_out: float32 [2, 768], replicated, may hold values from -3 to 3
- w_up: float32 [2, 768, 3072], P(None, None, 'tensor'), may hold values from -0.21875 to 0.21875
- b_up: float32 [2, 3072], P(None, 'tensor'), may hold values from -3 to 3
- w_down: float32 [2, 3072, 768], P(None, 'tensor'), may hold values from -0.109375 to 0.109375
- b_down: float32 [2, 768], replicated, may hold values from -3 to 3
- w_mod: float32 [2, 768, 4608], P(None, None, 'tensor'), may hold values from -0.21875 to 0.21875
- b_mod: float32 [2, 4608], P(None, 'tensor'), may hold values from -0.75 to 0.75
Outputs:
- outputs: float32 [16, 256, 768], P('dp')
- grad_inputs: float32 [16, 256, 768], P('dp')
- grad_condition: float32 [16, 768], P('dp')
- grad_w_qkv: float32 [2, 768, 3, 768], P(None, 'dp', None, 'tensor')
- grad_b_qv: float32 [2, 2, 768], P(None, None, 'tensor')
- grad_w_out: float32 [2, 768, 768], P(None, 'tensor', 'dp')
- grad_b_out: float32 [2, 768], replicated
- grad_w_up: float32 [2, 768, 3072], P(None, 'dp', 'tensor')
- grad_b_up: float32 [2, 3072], P(None, 'tensor')
- grad_w_down: float32 [2, 3072, 768], P(None, 'tensor', 'dp')
- grad_b_down: float32 [2, 768], replicated
- grad_w_mod: float32 [2, 768, 4608], P(None, 'dp', 'tensor')
- grad_b_mod: float32 [2, 4608], P(None, 'tensor')
The draws below stay inside these ranges and needn't reach their ends.
All inputs are finite; a program needn't handle non-finite values.
Results may differ from the reference program's by a relative error of at most 0.0003.
Values sent between devices are 32-bit elements; how exact they have to be, the bound alone decides.
A program may use at most 256 MiB of HBM per device.

```python
import jax
import jax.numpy as jnp
from jax import lax

D = 768
HEAD_DIM = 64
FF = 3072
SEQ = 256
LAYERS = 2
LATENTS = 16


def draw_condition(key, part):
    return jax.random.truncated_normal(key, -2.5, 2.5, (LATENTS, D), jnp.float32)


def draw_b_mod(key, part):
    return 0.3 * jax.random.truncated_normal(key, -2.5, 2.5, (LAYERS, 6 * D), jnp.float32)


def draw_b_qv(key, part):
    return 0.5 * jax.random.truncated_normal(key, -2.5, 2.5, (LAYERS, 2, D), jnp.float32)


def spiked(drawn, rng, source, target, blocks, factor):
    def block_of(axis_at):
        return (jnp.arange(drawn.shape[axis_at]) // (drawn.shape[axis_at] // blocks)).reshape((-1,) + (1,) * (drawn.ndim - 1 - axis_at))

    near = jax.random.permutation(rng, blocks)[block_of(target)]
    other_side = (block_of(target) + blocks // 2) % blocks
    return jnp.where((block_of(source) == near) | (block_of(source) == other_side), factor * drawn, drawn)


def steps_of(own_key, dims, shards, least, high):
    def one(position, parts):
        draws = jax.random.uniform(jax.random.fold_in(jax.random.fold_in(own_key, 6), position), (parts,), jnp.float32, least / len(shards), high / len(shards))
        return jnp.repeat(jnp.exp(draws), dims[position] // parts).reshape((-1,) + (1,) * (len(dims) - position - 1))

    level = one(*shards[0])
    for cut in shards[1:]:
        level = level * one(*cut)
    return level


def bell_draw(rng, extent, spread, bound, shards=(), dtype=jnp.bfloat16):
    factor_of = steps_of(rng, extent, shards, -0.22, 0.18) if shards else 1.0
    values = jax.random.normal(rng, extent, jnp.float32) * spread * factor_of
    return jnp.minimum(jnp.maximum(values, -bound), bound).astype(dtype)


def heavy_noise(stream_key, shape, spread, bound, cuts, heavy, held_as=jnp.bfloat16):
    entries = spread * jax.random.normal(stream_key, shape, jnp.float32)
    if cuts:
        entries = entries * steps_of(stream_key, shape, cuts, -0.22, 0.18)
    return jnp.clip(spiked(entries, jax.random.fold_in(stream_key, 3), *heavy), -bound, bound).astype(held_as)


def setup_inputs(seed: int = 0) -> dict:
    key_list = jax.random.split(jax.random.key(seed), 14)
    return {
        "inputs": bell_draw(key_list[0], (LATENTS, SEQ, D), 1.0, 6.0, ((0, 16),), jnp.float32),
        "condition": draw_condition(jax.random.fold_in(key_list[13], 71), 0),
        "cotangent": heavy_noise(key_list[2], (LATENTS, SEQ, D), 1.0, 6.0, ((0, 16),), (0, 2, 16, 2.0), jnp.float32),
        "w_qkv": bell_draw(key_list[3], (LAYERS, D, 3, D), D ** -0.5, 0.21875, ((3, 2),), jnp.float32),
        "b_qv": draw_b_qv(jax.random.fold_in(key_list[13], 71), 0),
        "w_out": bell_draw(key_list[5], (LAYERS, D, D), (D // 16) ** -0.5, 0.875, ((1, 2),), jnp.float32),
        "b_out": bell_draw(key_list[6], (LAYERS, D), 0.5, 3.0, (), jnp.float32),
        "w_up": bell_draw(key_list[7], (LAYERS, D, FF), D ** -0.5, 0.21875, ((2, 2),), jnp.float32),
        "b_up": bell_draw(key_list[8], (LAYERS, FF), 0.5, 3.0, ((1, 2),), jnp.float32),
        "w_down": bell_draw(key_list[9], (LAYERS, FF, D), FF ** -0.5, 0.109375, ((1, 2),), jnp.float32),
        "b_down": bell_draw(key_list[10], (LAYERS, D), 0.5, 3.0, (), jnp.float32),
        "w_mod": bell_draw(key_list[11], (LAYERS, D, 6 * D), D ** -0.5, 0.21875, ((2, 2),), jnp.float32),
        "b_mod": draw_b_mod(jax.random.fold_in(key_list[13], 71), 0),
    }


@jax.custom_vjp
def low(v):
    return lax.optimization_barrier(v.astype(jnp.bfloat16)).astype(jnp.float32)

@jax.custom_vjp
def low_back(v):
    return v

def low_keep(v):
    return (low(v), None)

def low_pass(kept, grad):
    return (grad,)

def back_keep(v):
    return (v, None)

def back_low(kept, grad):
    return (low(grad),)
low.defvjp(low_keep, low_pass)
low_back.defvjp(back_keep, back_low)
highest = lax.Precision.HIGHEST
eps_norm = 1e-06

def layer_norm(values):
    row_mean = lax.optimization_barrier(jnp.mean(values, axis=-1, keepdims=True))
    centred = values - row_mean
    row_var = lax.optimization_barrier(jnp.mean(centred * centred, axis=-1, keepdims=True))
    return centred * lax.rsqrt(row_var + eps_norm)

def forward(inputs, condition, weights):
    w_qkv, b_qv, w_out, b_out, w_up, b_up, w_down, b_down, w_mod, b_mod = weights
    batch, seq_len, width = inputs.shape
    heads = width // HEAD_DIM
    score_scale = HEAD_DIM ** (-0.5)
    activated = jax.nn.silu(condition)
    hidden = inputs
    for layer_index in range(LAYERS):
        modulation = (jnp.dot(activated, w_mod[layer_index], precision=highest) + b_mod[layer_index]).reshape(batch, 6, width)
        shift_a, scale_a, gate_a = (modulation[:, 0], modulation[:, 1], modulation[:, 2])
        shift_b, scale_b, gate_b = (modulation[:, 3], modulation[:, 4], modulation[:, 5])
        modul_a = layer_norm(hidden) * (1.0 + scale_a[:, None, :]) + shift_a[:, None, :]
        projected = jnp.einsum('bsd,dcm->bscm', modul_a, w_qkv[layer_index], precision=highest)
        queries = (projected[:, :, 0] + b_qv[layer_index, 0]).reshape(batch, seq_len, heads, HEAD_DIM)
        keys = projected[:, :, 1].reshape(batch, seq_len, heads, HEAD_DIM)
        values = (projected[:, :, 2] + b_qv[layer_index, 1]).reshape(batch, seq_len, heads, HEAD_DIM)
        scores = jnp.einsum('bqhe,bkhe->bhqk', queries, keys, precision=highest) * score_scale
        probs = jax.nn.softmax(scores, axis=-1)
        attended = jnp.einsum('bhqk,bkhe->bqhe', probs, values, precision=highest).reshape(batch, seq_len, width)
        attn_branch = jnp.einsum('bsh,hd->bsd', attended, w_out[layer_index], precision=highest) + b_out[layer_index]
        middle = hidden + gate_a[:, None, :] * attn_branch
        modul_b = layer_norm(middle) * (1.0 + scale_b[:, None, :]) + shift_b[:, None, :]
        pre_act = jnp.einsum('bsd,df->bsf', modul_b, w_up[layer_index], precision=highest) + b_up[layer_index]
        activ = jax.nn.gelu(pre_act, approximate=True)
        mlp_branch = jnp.einsum('bsf,fd->bsd', activ, w_down[layer_index], precision=highest) + b_down[layer_index]
        hidden = middle + gate_b[:, None, :] * mlp_branch
    return hidden

def reference(inputs, condition, cotangent, w_qkv, b_qv, w_out, b_out, w_up, b_up, w_down, b_down, w_mod, b_mod):
    weights = (w_qkv, b_qv, w_out, b_out, w_up, b_up, w_down, b_down, w_mod, b_mod)
    group_size = min(16, LATENTS)
    groups = LATENTS // group_size
    tokens_grouped = inputs.reshape(groups, group_size, SEQ, D)
    cond_grouped = condition.reshape(groups, group_size, D)
    cot_grouped = cotangent.reshape(groups, group_size, SEQ, D)

    def one_group(running, pieces):
        token_part, cond_part, cot_part = pieces
        result, pullback = jax.vjp(forward, token_part, cond_part, weights)
        grad_tokens, grad_cond, grad_weights = pullback(cot_part)
        running = jax.tree.map(lambda left, right: left + right, running, grad_weights)
        return (running, (result, grad_tokens, grad_cond))
    zeros = jax.tree.map(jnp.zeros_like, weights)
    summed, (results, grad_tokens, grad_cond) = lax.scan(one_group, zeros, (tokens_grouped, cond_grouped, cot_grouped))
    return (results.reshape(LATENTS, SEQ, D), grad_tokens.reshape(LATENTS, SEQ, D), grad_cond.reshape(LATENTS, D), summed[0], summed[1], summed[2], summed[3], summed[4], summed[5], summed[6], summed[7], summed[8], summed[9])
```

```python
import jax
import jax.numpy as jnp
from jax import lax
from jax.sharding import PartitionSpec as P

HEAD_DIM = 64


high = lax.Precision.HIGH
eps_norm = 1e-06


def layer_norm(values):
    row_mean = jnp.mean(values, axis=-1, keepdims=True)
    centred = values - row_mean
    row_var = jnp.mean(centred * centred, axis=-1, keepdims=True)
    return centred * lax.rsqrt(row_var + eps_norm)


def gelu_tanh(values):
    return jax.nn.gelu(values, approximate=True)


def silu_slope(values):
    sigma = jax.nn.sigmoid(values)
    return sigma * (1.0 + values * (1.0 - sigma))


def pair_sum(value):
    if lax.axis_size("tensor") == 2:
        return value + lax.ppermute(value, "tensor", [(0, 1), (1, 0)])
    return lax.psum(value, "tensor")


def pair_gather(value, axis):
    if lax.axis_size("tensor") == 2:
        other = lax.ppermute(value, "tensor", [(0, 1), (1, 0)])
        first = lax.axis_index("tensor") == 0
        low = jnp.where(first, value, other)
        top = jnp.where(first, other, value)
        return jnp.concatenate([low, top], axis=axis)
    return lax.all_gather(value, "tensor", axis=axis, tiled=True)


def vec_mat(vec, mat):
    if vec.shape[0] == 1:
        return jnp.sum(vec[0][:, None] * mat, axis=0)[None]
    return jnp.einsum("bk,km->bm", vec, mat, precision=high)


def vec_mat_t(vec, mat):
    if vec.shape[0] == 1:
        return jnp.sum(vec[0][None, :] * mat, axis=1)[None]
    return jnp.einsum("bm,km->bk", vec, mat, precision=high)


def scattered_grad(left, right):
    tokens = left.shape[0] * left.shape[1]
    rows = left.shape[2]
    cols = right.shape[2]
    left_t = left.reshape(tokens, rows).T
    right = right.reshape(tokens, cols)
    count = lax.axis_size("dp")
    if count & (count - 1) or count < 2:
        whole = jnp.dot(left_t, right, precision=high)
        return lax.psum_scatter(whole, "dp", scatter_dimension=0, tiled=True)
    block = rows // count
    index = lax.axis_index("dp")
    bit = index % 2
    blocks = left_t.reshape(count // 2, 2, block, tokens)

    def product(which):
        chosen = lax.dynamic_index_in_dim(blocks, which, 1, keepdims=False)
        return jnp.dot(chosen.reshape(rows // 2, tokens), right, precision=high)

    pairs = [(device, device ^ 1) for device in range(count)]
    arrived = lax.ppermute(product(1 - bit), "dp", pairs)
    total = product(bit) + arrived
    step = 2
    groups = count // 2
    while groups > 1:
        bit = (index // step) % 2
        parts = total.reshape(groups // 2, 2, block, cols)
        away = lax.dynamic_index_in_dim(parts, 1 - bit, 1, keepdims=False)
        kept = lax.dynamic_index_in_dim(parts, bit, 1, keepdims=False)
        pairs = [(device, device ^ step) for device in range(count)]
        total = kept + lax.ppermute(away, "dp", pairs)
        groups //= 2
        step *= 2
    return total.reshape(block, cols)

def on_device(
    inputs,
    condition,
    cotangent,
    w_qkv,
    b_qv,
    w_out,
    b_out,
    w_up,
    b_up,
    w_down,
    b_down,
    w_mod,
    b_mod,
):
    layers = w_qkv.shape[0]
    batch, seq_len, width = inputs.shape
    local_width = w_qkv.shape[3]
    heads_local = local_width // HEAD_DIM
    mod_cols = w_mod.shape[2]
    score_scale = HEAD_DIM ** (-0.5)
    activated = jax.nn.silu(condition)
    mod_local = (
        jnp.stack([vec_mat(activated, w_mod[index]) for index in range(layers)], axis=0)
        + b_mod[:, None, :]
    )
    mod_whole = pair_gather(mod_local, 2).reshape(layers, batch, 6, width)
    activated_all = lax.all_gather(activated, "dp", axis=0, tiled=True)
    kept = []
    hidden = inputs
    for layer_index in range(layers):
        modulation = mod_whole[layer_index]
        shift_a, scale_a, gate_a = (modulation[:, 0], modulation[:, 1], modulation[:, 2])
        shift_b, scale_b, gate_b = (modulation[:, 3], modulation[:, 4], modulation[:, 5])
        modul_a = layer_norm(hidden) * (1.0 + scale_a[:, None, :]) + shift_a[:, None, :]
        projected = jnp.einsum("bsd,dcm->bscm", modul_a, w_qkv[layer_index], precision=high)
        queries = (projected[:, :, 0] + b_qv[layer_index, 0]).reshape(
            batch, seq_len, heads_local, HEAD_DIM
        )
        keys = projected[:, :, 1].reshape(batch, seq_len, heads_local, HEAD_DIM)
        values = (projected[:, :, 2] + b_qv[layer_index, 1]).reshape(
            batch, seq_len, heads_local, HEAD_DIM
        )
        scores = jnp.einsum("bqhe,bkhe->bhqk", queries, keys, precision=high) * score_scale
        log_norm = jax.nn.logsumexp(scores, axis=-1, keepdims=True)
        probs = jnp.exp(scores - log_norm)
        attended = jnp.einsum("bhqk,bkhe->bqhe", probs, values, precision=high).reshape(
            batch, seq_len, local_width
        )
        partial_a = jnp.einsum("bsh,hd->bsd", attended, w_out[layer_index], precision=high)
        attn_branch = pair_sum(partial_a) + b_out[layer_index]
        middle = hidden + gate_a[:, None, :] * attn_branch
        modul_b = layer_norm(middle) * (1.0 + scale_b[:, None, :]) + shift_b[:, None, :]
        pre_act = (
            jnp.einsum("bsd,df->bsf", modul_b, w_up[layer_index], precision=high)
            + b_up[layer_index]
        )
        activ = gelu_tanh(pre_act)
        partial_b = jnp.einsum("bsf,fd->bsd", activ, w_down[layer_index], precision=high)
        mlp_branch = pair_sum(partial_b) + b_down[layer_index]
        result = middle + gate_b[:, None, :] * mlp_branch
        kept.append(
            (
                hidden,
                modul_a,
                queries,
                keys,
                values,
                probs,
                attended,
                attn_branch,
                middle,
                modul_b,
                pre_act,
                activ,
                mlp_branch,
            )
        )
        hidden = result
    grad_hidden = cotangent
    silu_grad_part = jnp.zeros((batch, width), jnp.float32)
    matrix_grads = [None] * layers
    pieces = [None] * layers
    for layer_index in reversed(range(layers)):
        (
            layer_in,
            modul_a,
            queries,
            keys,
            values,
            probs,
            attended,
            attn_branch,
            middle,
            modul_b,
            pre_act,
            activ,
            mlp_branch,
        ) = kept[layer_index]
        modulation = mod_whole[layer_index]
        scale_a, gate_a = (modulation[:, 1], modulation[:, 2])
        scale_b, gate_b = (modulation[:, 4], modulation[:, 5])
        d_branch_b = grad_hidden * gate_b[:, None, :]
        d_gate_b = jnp.sum(grad_hidden * mlp_branch, axis=1)
        g_b_down = jnp.sum(d_branch_b, axis=(0, 1))
        g_w_down = scattered_grad(d_branch_b, activ)
        d_activ = jnp.einsum("bsd,fd->bsf", d_branch_b, w_down[layer_index], precision=high)
        d_pre = jax.vjp(gelu_tanh, pre_act)[1](d_activ)[0]
        g_b_up = jnp.sum(d_pre, axis=(0, 1))
        g_w_up = scattered_grad(modul_b, d_pre)
        d_modul_b = pair_sum(
            jnp.einsum("bsf,df->bsd", d_pre, w_up[layer_index], precision=high)
        )
        normed_b, norm_back_b = jax.vjp(layer_norm, middle)
        d_scale_b = jnp.sum(d_modul_b * normed_b, axis=1)
        d_shift_b = jnp.sum(d_modul_b, axis=1)
        d_middle = grad_hidden + norm_back_b(d_modul_b * (1.0 + scale_b[:, None, :]))[0]
        d_branch_a = d_middle * gate_a[:, None, :]
        d_gate_a = jnp.sum(d_middle * attn_branch, axis=1)
        g_b_out = jnp.sum(d_branch_a, axis=(0, 1))
        g_w_out = scattered_grad(d_branch_a, attended)
        d_attended = jnp.einsum(
            "bsd,hd->bsh", d_branch_a, w_out[layer_index], precision=high
        ).reshape(batch, seq_len, heads_local, HEAD_DIM)
        d_values = jnp.einsum("bhqk,bqhe->bkhe", probs, d_attended, precision=high)
        d_probs = jnp.einsum("bqhe,bkhe->bhqk", d_attended, values, precision=high)
        attended_heads = attended.reshape(batch, seq_len, heads_local, HEAD_DIM)
        row_dot = jnp.transpose(jnp.sum(d_attended * attended_heads, axis=-1), (0, 2, 1))[..., None]
        d_scores = probs * (d_probs - row_dot) * score_scale
        d_queries = jnp.einsum("bhqk,bkhe->bqhe", d_scores, keys, precision=high)
        d_keys = jnp.einsum("bhqk,bqhe->bkhe", d_scores, queries, precision=high)
        d_proj = jnp.stack([d_queries, d_keys, d_values], axis=2).reshape(
            batch, seq_len, 3, local_width
        )
        d_flat = d_proj.reshape(batch, seq_len, 3 * local_width)
        g_b_qv = jnp.sum(d_flat, axis=(0, 1))
        g_w_qkv = scattered_grad(modul_a, d_flat)
        d_modul_a = pair_sum(
            jnp.einsum("bscm,dcm->bsd", d_proj, w_qkv[layer_index], precision=high)
        )
        normed_a, norm_back_a = jax.vjp(layer_norm, layer_in)
        d_scale_a = jnp.sum(d_modul_a * normed_a, axis=1)
        d_shift_a = jnp.sum(d_modul_a, axis=1)
        grad_hidden = d_middle + norm_back_a(d_modul_a * (1.0 + scale_a[:, None, :]))[0]
        d_mod = jnp.stack(
            [d_shift_a, d_scale_a, d_gate_a, d_shift_b, d_scale_b, d_gate_b], axis=1
        ).reshape(batch, 6 * width)
        own_cols = lax.dynamic_slice_in_dim(d_mod, lax.axis_index("tensor") * mod_cols, mod_cols, 1)
        silu_grad_part = silu_grad_part + vec_mat_t(own_cols, w_mod[layer_index])
        matrix_grads[layer_index] = (g_w_qkv, g_w_out, g_w_up, g_w_down)
        pieces[layer_index] = (own_cols, (g_b_qv, g_b_out, g_b_up, g_b_down))
    block = width // lax.axis_size("dp")
    activated_rows = lax.dynamic_slice_in_dim(
        activated_all, lax.axis_index("dp") * block, block, 1
    )
    mod_grads = [None] * layers
    bias_grads = [None] * layers
    for layer_index in reversed(range(layers)):
        own_cols, biases = pieces[layer_index]
        line = jnp.concatenate(biases)[None]
        line = jnp.concatenate([line, jnp.zeros((batch - 1, line.shape[1]), line.dtype)], axis=0)
        gathered = lax.all_gather(
            jnp.concatenate([own_cols, line], axis=1), "dp", axis=0, tiled=True
        )
        mod_grads[layer_index] = jnp.einsum(
            "bd,bm->dm", activated_rows, gathered[:, :mod_cols], precision=high
        )
        sums = jnp.sum(gathered, axis=0)
        found = [sums[:mod_cols]]
        start = mod_cols
        for piece in biases:
            found.append(sums[start : start + piece.shape[0]])
            start += piece.shape[0]
        bias_grads[layer_index] = found
    order = range(layers)
    grad_w_qkv = jnp.stack([matrix_grads[index][0] for index in order], axis=0)
    grad_w_out = jnp.stack([matrix_grads[index][1].T for index in order], axis=0)
    grad_w_up = jnp.stack([matrix_grads[index][2] for index in order], axis=0)
    grad_w_down = jnp.stack([matrix_grads[index][3].T for index in order], axis=0)
    grad_b_mod, grad_b_qkv, grad_b_out, grad_b_up, grad_b_down = [
        jnp.stack([bias_grads[index][member] for index in order], axis=0) for member in range(5)
    ]
    grad_b_qv = grad_b_qkv.reshape(layers, 3, local_width)[:, ::2]
    grad_condition = pair_sum(silu_grad_part) * silu_slope(condition)
    return (
        hidden,
        grad_hidden,
        grad_condition,
        grad_w_qkv.reshape(layers, block, 3, local_width),
        grad_b_qv,
        grad_w_out,
        grad_b_out,
        grad_w_up,
        grad_b_up,
        grad_w_down,
        grad_b_down,
        jnp.stack(mod_grads, axis=0),
        grad_b_mod,
    )


def solution(mesh):
    in_specs = (
        P("dp", None, None),
        P("dp", None),
        P("dp", None, None),
        P(None, None, None, "tensor"),
        P(None, None, "tensor"),
        P(None, "tensor", None),
        P(),
        P(None, None, "tensor"),
        P(None, "tensor"),
        P(None, "tensor", None),
        P(),
        P(None, None, "tensor"),
        P(None, "tensor"),
    )
    out_specs = (
        P("dp", None, None),
        P("dp", None, None),
        P("dp", None),
        P(None, "dp", None, "tensor"),
        P(None, None, "tensor"),
        P(None, "tensor", "dp"),
        P(),
        P(None, "dp", "tensor"),
        P(None, "tensor"),
        P(None, "tensor", "dp"),
        P(),
        P(None, "dp", "tensor"),
        P(None, "tensor"),
    )
    return jax.shard_map(
        on_device, mesh=mesh, in_specs=in_specs, out_specs=out_specs, check_vma=False
    )
```

```python
import jax
import jax.numpy as jnp
from jax import lax
from jax.sharding import PartitionSpec as P

HEAD_DIM = 64


high = lax.Precision.HIGH
eps_norm = 1e-06


def layer_norm(values):
    row_mean = jnp.mean(values, axis=-1, keepdims=True)
    centred = values - row_mean
    row_var = jnp.mean(centred * centred, axis=-1, keepdims=True)
    return centred * lax.rsqrt(row_var + eps_norm)


def gelu_tanh(values):
    return jax.nn.gelu(values, approximate=True)


def silu_slope(values):
    sigma = jax.nn.sigmoid(values)
    return sigma * (1.0 + values * (1.0 - sigma))


def pair_sum(value):
    if lax.axis_size("tensor") == 2:
        return value + lax.ppermute(value, "tensor", [(0, 1), (1, 0)])
    return lax.psum(value, "tensor")


def pair_gather(value, axis):
    if lax.axis_size("tensor") == 2:
        other = lax.ppermute(value, "tensor", [(0, 1), (1, 0)])
        first = lax.axis_index("tensor") == 0
        low = jnp.where(first, value, other)
        top = jnp.where(first, other, value)
        return jnp.concatenate([low, top], axis=axis)
    return lax.all_gather(value, "tensor", axis=axis, tiled=True)


def vec_mat(vec, mat):
    if vec.shape[0] == 1:
        return jnp.sum(vec[0][:, None] * mat, axis=0)[None]
    return jnp.einsum("bk,km->bm", vec, mat, precision=high)


def vec_mat_t(vec, mat):
    if vec.shape[0] == 1:
        return jnp.sum(vec[0][None, :] * mat, axis=1)[None]
    return jnp.einsum("bm,km->bk", vec, mat, precision=high)


class GradScatter:
    def __init__(self, left, right):
        tokens = left.shape[0] * left.shape[1]
        rows, self.cols = left.shape[2], right.shape[2]
        count = lax.axis_size("dp")
        self.block = rows // count
        whole = jnp.einsum(
            "td,tc->dc",
            left.reshape(tokens, rows),
            right.reshape(tokens, self.cols),
            precision=high,
        )
        self.flight = None
        if count & (count - 1):
            self.total = lax.psum_scatter(whole, "dp", scatter_dimension=0, tiled=True)
        else:
            self.total = whole
            self.step, self.groups = 1, count
            self.launch(self.split())

    def split(self):
        if self.groups == 1:
            self.flight = None
            return None
        bit = (lax.axis_index("dp") // self.step) % 2
        parts = self.total.reshape(self.groups // 2, 2, self.block, self.cols)
        self.kept = lax.dynamic_index_in_dim(parts, bit, 1, keepdims=False)
        return lax.dynamic_index_in_dim(parts, 1 - bit, 1, keepdims=False)

    def add(self, arrived):
        self.total = self.kept + arrived
        self.step *= 2
        self.groups //= 2
        return self.split()

    def launch(self, away):
        if away is not None:
            pairs = [(device, device ^ self.step) for device in range(lax.axis_size("dp"))]
            self.flight = lax.ppermute(away, "dp", pairs)

    def result(self):
        while self.flight is not None:
            self.launch(self.add(self.flight))
        return self.total.reshape(self.block, self.cols)


class RowGather:
    def __init__(self, row):
        count = lax.axis_size("dp")
        self.total = row[None]
        self.flight = None
        if count & (count - 1):
            self.total = lax.all_gather(row, "dp", axis=0, tiled=False)
        else:
            self.step = count
            self.launch(self.split())

    def split(self):
        self.step //= 2
        if self.step == 0:
            self.flight = None
            return None
        return self.total

    def add(self, arrived):
        first = (lax.axis_index("dp") // self.step) % 2 == 0
        low = jnp.where(first, self.total, arrived)
        top = jnp.where(first, arrived, self.total)
        both = jnp.stack([low, top], axis=1)
        self.total = both.reshape((both.shape[0] * 2,) + both.shape[2:])
        return self.split()

    def launch(self, away):
        if away is not None:
            pairs = [(device, device ^ self.step) for device in range(lax.axis_size("dp"))]
            self.flight = lax.ppermute(away, "dp", pairs)

    def result(self):
        while self.flight is not None:
            self.launch(self.add(self.flight))
        return self.total.reshape((-1, self.total.shape[-1]))


def tick(critical, tasks):
    live = [task for task in tasks if task.flight is not None]
    if not live:
        return critical
    critical, *landed = lax.optimization_barrier((critical, *[task.flight for task in live]))
    away = [task.add(value) for task, value in zip(live, landed)]
    more = [(task, value) for task, value in zip(live, away) if value is not None]
    if more:
        critical, *ready = lax.optimization_barrier((critical, *[value for _, value in more]))
        for (task, _), value in zip(more, ready):
            task.launch(value)
    return critical


def on_device(
    inputs,
    condition,
    cotangent,
    w_qkv,
    b_qv,
    w_out,
    b_out,
    w_up,
    b_up,
    w_down,
    b_down,
    w_mod,
    b_mod,
):
    layers = w_qkv.shape[0]
    batch, seq_len, width = inputs.shape
    local_width = w_qkv.shape[3]
    heads_local = local_width // HEAD_DIM
    mod_cols = w_mod.shape[2]
    score_scale = HEAD_DIM ** (-0.5)
    activated = jax.nn.silu(condition)
    mod_local = (
        jnp.stack([vec_mat(activated, w_mod[index]) for index in range(layers)], axis=0)
        + b_mod[:, None, :]
    )
    mod_whole = pair_gather(mod_local, 2).reshape(layers, batch, 6, width)
    condition_task = RowGather(activated)
    kept = []
    hidden = inputs
    for layer_index in range(layers):
        modulation = mod_whole[layer_index]
        shift_a, scale_a, gate_a = (modulation[:, 0], modulation[:, 1], modulation[:, 2])
        shift_b, scale_b, gate_b = (modulation[:, 3], modulation[:, 4], modulation[:, 5])
        modul_a = layer_norm(hidden) * (1.0 + scale_a[:, None, :]) + shift_a[:, None, :]
        modul_a = lax.optimization_barrier(modul_a)
        projected = jnp.einsum("bsd,dcm->bscm", modul_a, w_qkv[layer_index], precision=high)
        queries = (projected[:, :, 0] + b_qv[layer_index, 0]).reshape(
            batch, seq_len, heads_local, HEAD_DIM
        )
        keys = projected[:, :, 1].reshape(batch, seq_len, heads_local, HEAD_DIM)
        values = (projected[:, :, 2] + b_qv[layer_index, 1]).reshape(
            batch, seq_len, heads_local, HEAD_DIM
        )
        scores = jnp.einsum("bqhe,bkhe->bhqk", queries, keys, precision=high) * score_scale
        log_norm = jax.nn.logsumexp(scores, axis=-1, keepdims=True)
        probs = jnp.exp(scores - log_norm)
        attended = jnp.einsum("bhqk,bkhe->bqhe", probs, values, precision=high).reshape(
            batch, seq_len, local_width
        )
        partial_a = jnp.einsum("bsh,hd->bsd", attended, w_out[layer_index], precision=high)
        attn_branch = pair_sum(partial_a) + b_out[layer_index]
        middle = hidden + gate_a[:, None, :] * attn_branch
        modul_b = layer_norm(middle) * (1.0 + scale_b[:, None, :]) + shift_b[:, None, :]
        modul_b = lax.optimization_barrier(modul_b)
        pre_act = (
            jnp.einsum("bsd,df->bsf", modul_b, w_up[layer_index], precision=high)
            + b_up[layer_index]
        )
        activ = gelu_tanh(pre_act)
        partial_b = jnp.einsum("bsf,fd->bsd", activ, w_down[layer_index], precision=high)
        mlp_branch = pair_sum(partial_b) + b_down[layer_index]
        result = middle + gate_b[:, None, :] * mlp_branch
        kept.append(
            (
                hidden,
                modul_a,
                queries,
                keys,
                values,
                probs,
                attended,
                attn_branch,
                middle,
                modul_b,
                pre_act,
                activ,
                mlp_branch,
            )
        )
        hidden = result
    grad_hidden = cotangent
    silu_grad_part = jnp.zeros((batch, width), jnp.float32)
    matrix_grads = [None] * layers
    pieces = [None] * layers
    older = [condition_task]
    for layer_index in reversed(range(layers)):
        (
            layer_in,
            modul_a,
            queries,
            keys,
            values,
            probs,
            attended,
            attn_branch,
            middle,
            modul_b,
            pre_act,
            activ,
            mlp_branch,
        ) = kept[layer_index]
        modulation = mod_whole[layer_index]
        scale_a, gate_a = (modulation[:, 1], modulation[:, 2])
        scale_b, gate_b = (modulation[:, 4], modulation[:, 5])
        d_branch_b = grad_hidden * gate_b[:, None, :]
        d_gate_b = jnp.sum(grad_hidden * mlp_branch, axis=1)
        g_b_down = jnp.sum(d_branch_b, axis=(0, 1))
        g_w_down = GradScatter(d_branch_b, activ)
        d_activ = jnp.einsum("bsd,fd->bsf", d_branch_b, w_down[layer_index], precision=high)
        d_pre = jax.vjp(gelu_tanh, pre_act)[1](d_activ)[0]
        d_pre = tick(d_pre, older + [g_w_down])
        g_b_up = jnp.sum(d_pre, axis=(0, 1))
        g_w_up = GradScatter(modul_b, d_pre)
        d_modul_b = pair_sum(
            jnp.einsum("bsf,df->bsd", d_pre, w_up[layer_index], precision=high)
        )
        d_modul_b = tick(d_modul_b, older + [g_w_up])
        normed_b, norm_back_b = jax.vjp(layer_norm, middle)
        d_scale_b = jnp.sum(d_modul_b * normed_b, axis=1)
        d_shift_b = jnp.sum(d_modul_b, axis=1)
        d_middle = grad_hidden + norm_back_b(d_modul_b * (1.0 + scale_b[:, None, :]))[0]
        d_branch_a = d_middle * gate_a[:, None, :]
        d_gate_a = jnp.sum(d_middle * attn_branch, axis=1)
        g_b_out = jnp.sum(d_branch_a, axis=(0, 1))
        g_w_out = GradScatter(d_branch_a, attended)
        d_attended = jnp.einsum(
            "bsd,hd->bsh", d_branch_a, w_out[layer_index], precision=high
        ).reshape(batch, seq_len, heads_local, HEAD_DIM)
        d_values = jnp.einsum("bhqk,bqhe->bkhe", probs, d_attended, precision=high)
        d_probs = jnp.einsum("bqhe,bkhe->bhqk", d_attended, values, precision=high)
        attended_heads = attended.reshape(batch, seq_len, heads_local, HEAD_DIM)
        row_dot = jnp.transpose(jnp.sum(d_attended * attended_heads, axis=-1), (0, 2, 1))[..., None]
        d_scores = probs * (d_probs - row_dot) * score_scale
        d_scores = tick(d_scores, older + [g_w_down, g_w_out])
        d_queries = jnp.einsum("bhqk,bkhe->bqhe", d_scores, keys, precision=high)
        d_keys = jnp.einsum("bhqk,bqhe->bkhe", d_scores, queries, precision=high)
        d_proj = jnp.stack([d_queries, d_keys, d_values], axis=2).reshape(
            batch, seq_len, 3, local_width
        )
        d_flat = d_proj.reshape(batch, seq_len, 3 * local_width)
        g_b_qv = jnp.sum(d_flat, axis=(0, 1))
        g_w_qkv = GradScatter(modul_a, d_flat)
        d_modul_a = pair_sum(
            jnp.einsum("bscm,dcm->bsd", d_proj, w_qkv[layer_index], precision=high)
        )
        d_modul_a = tick(d_modul_a, older + [g_w_down, g_w_up, g_w_out, g_w_qkv])
        normed_a, norm_back_a = jax.vjp(layer_norm, layer_in)
        d_scale_a = jnp.sum(d_modul_a * normed_a, axis=1)
        d_shift_a = jnp.sum(d_modul_a, axis=1)
        grad_hidden = d_middle + norm_back_a(d_modul_a * (1.0 + scale_a[:, None, :]))[0]
        d_mod = jnp.stack(
            [d_shift_a, d_scale_a, d_gate_a, d_shift_b, d_scale_b, d_gate_b], axis=1
        ).reshape(batch, 6 * width)
        own_cols = lax.dynamic_slice_in_dim(d_mod, lax.axis_index("tensor") * mod_cols, mod_cols, 1)
        silu_grad_part = silu_grad_part + vec_mat_t(own_cols, w_mod[layer_index])
        matrix_grads[layer_index] = (g_w_qkv, g_w_out, g_w_up, g_w_down)
        biases = (g_b_qv, g_b_out, g_b_up, g_b_down)
        line = jnp.concatenate(biases)[None]
        line = jnp.concatenate([line, jnp.zeros((batch - 1, line.shape[1]), line.dtype)], axis=0)
        rows_task = RowGather(jnp.concatenate([own_cols, line], axis=1))
        pieces[layer_index] = (rows_task, biases)
        older = [g_w_down, g_w_up, g_w_out, g_w_qkv, rows_task]
    block = width // lax.axis_size("dp")
    activated_rows = lax.dynamic_slice_in_dim(
        condition_task.result(), lax.axis_index("dp") * block, block, 1
    )
    mod_grads = [None] * layers
    bias_grads = [None] * layers
    for layer_index in reversed(range(layers)):
        rows_task, biases = pieces[layer_index]
        gathered = rows_task.result()
        mod_grads[layer_index] = jnp.einsum(
            "bd,bm->dm", activated_rows, gathered[:, :mod_cols], precision=high
        )
        sums = jnp.sum(gathered, axis=0)
        found = [sums[:mod_cols]]
        start = mod_cols
        for piece in biases:
            found.append(sums[start : start + piece.shape[0]])
            start += piece.shape[0]
        bias_grads[layer_index] = found
    order = range(layers)
    grad_w_qkv = jnp.stack([matrix_grads[index][0].result() for index in order], axis=0)
    grad_w_out = jnp.stack([matrix_grads[index][1].result().T for index in order], axis=0)
    grad_w_up = jnp.stack([matrix_grads[index][2].result() for index in order], axis=0)
    grad_w_down = jnp.stack([matrix_grads[index][3].result().T for index in order], axis=0)
    grad_b_mod, grad_b_qkv, grad_b_out, grad_b_up, grad_b_down = [
        jnp.stack([bias_grads[index][member] for index in order], axis=0) for member in range(5)
    ]
    grad_b_qv = grad_b_qkv.reshape(layers, 3, local_width)[:, ::2]
    grad_condition = pair_sum(silu_grad_part) * silu_slope(condition)
    return (
        hidden,
        grad_hidden,
        grad_condition,
        grad_w_qkv.reshape(layers, block, 3, local_width),
        grad_b_qv,
        grad_w_out,
        grad_b_out,
        grad_w_up,
        grad_b_up,
        grad_w_down,
        grad_b_down,
        jnp.stack(mod_grads, axis=0),
        grad_b_mod,
    )


def solution(mesh):
    in_specs = (
        P("dp", None, None),
        P("dp", None),
        P("dp", None, None),
        P(None, None, None, "tensor"),
        P(None, None, "tensor"),
        P(None, "tensor", None),
        P(),
        P(None, None, "tensor"),
        P(None, "tensor"),
        P(None, "tensor", None),
        P(),
        P(None, None, "tensor"),
        P(None, "tensor"),
    )
    out_specs = (
        P("dp", None, None),
        P("dp", None, None),
        P("dp", None),
        P(None, "dp", None, "tensor"),
        P(None, None, "tensor"),
        P(None, "tensor", "dp"),
        P(),
        P(None, "dp", "tensor"),
        P(None, "tensor"),
        P(None, "tensor", "dp"),
        P(),
        P(None, "dp", "tensor"),
        P(None, "tensor"),
    )
    return jax.shard_map(
        on_device, mesh=mesh, in_specs=in_specs, out_specs=out_specs, check_vma=False
    )
```

```python
import jax
import jax.numpy as jnp
from jax import lax
from jax.sharding import PartitionSpec as P

HEAD_DIM = 64


high = lax.Precision.HIGH
eps_norm = 1e-06


def layer_norm(values):
    row_mean = jnp.mean(values, axis=-1, keepdims=True)
    centred = values - row_mean
    row_var = jnp.mean(centred * centred, axis=-1, keepdims=True)
    return centred * lax.rsqrt(row_var + eps_norm)


def gelu_tanh(values):
    return jax.nn.gelu(values, approximate=True)


def silu_slope(values):
    sigma = jax.nn.sigmoid(values)
    return sigma * (1.0 + values * (1.0 - sigma))


def pair_sum(value):
    if lax.axis_size("tensor") == 2:
        return value + lax.ppermute(value, "tensor", [(0, 1), (1, 0)])
    return lax.psum(value, "tensor")


def pair_gather(value, axis):
    if lax.axis_size("tensor") == 2:
        other = lax.ppermute(value, "tensor", [(0, 1), (1, 0)])
        first = lax.axis_index("tensor") == 0
        low = jnp.where(first, value, other)
        top = jnp.where(first, other, value)
        return jnp.concatenate([low, top], axis=axis)
    return lax.all_gather(value, "tensor", axis=axis, tiled=True)


def vec_mat(vec, mat):
    if vec.shape[0] == 1:
        return jnp.sum(vec[0][:, None] * mat, axis=0)[None]
    return jnp.einsum("bk,km->bm", vec, mat, precision=high)


def vec_mat_t(vec, mat):
    if vec.shape[0] == 1:
        return jnp.sum(vec[0][None, :] * mat, axis=1)[None]
    return jnp.einsum("bm,km->bk", vec, mat, precision=high)


class GradScatter:
    def __init__(self, left, right):
        tokens = left.shape[0] * left.shape[1]
        rows, self.cols = left.shape[2], right.shape[2]
        count = lax.axis_size("dp")
        self.block = rows // count
        whole = jnp.einsum(
            "td,tc->dc",
            left.reshape(tokens, rows),
            right.reshape(tokens, self.cols),
            precision=high,
        )
        self.flight = None
        if count & (count - 1):
            self.total = lax.psum_scatter(whole, "dp", scatter_dimension=0, tiled=True)
        else:
            self.total = whole
            self.step, self.groups = 1, count
            self.launch(self.split())

    def split(self):
        if self.groups == 1:
            self.flight = None
            return None
        bit = (lax.axis_index("dp") // self.step) % 2
        parts = self.total.reshape(self.groups // 2, 2, self.block, self.cols)
        self.kept = lax.dynamic_index_in_dim(parts, bit, 1, keepdims=False)
        return lax.dynamic_index_in_dim(parts, 1 - bit, 1, keepdims=False)

    def add(self, arrived):
        self.total = self.kept + arrived
        self.step *= 2
        self.groups //= 2
        return self.split()

    def launch(self, away):
        if away is not None:
            pairs = [(device, device ^ self.step) for device in range(lax.axis_size("dp"))]
            self.flight = lax.ppermute(away, "dp", pairs)

    def result(self):
        while self.flight is not None:
            self.launch(self.add(self.flight))
        return self.total.reshape(self.block, self.cols)


class RowGather:
    def __init__(self, row):
        count = lax.axis_size("dp")
        self.total = row[None]
        self.flight = None
        if count & (count - 1):
            self.total = lax.all_gather(row, "dp", axis=0, tiled=False)
        else:
            self.step = count
            self.launch(self.split())

    def split(self):
        self.step //= 2
        if self.step == 0:
            self.flight = None
            return None
        self.kept = self.total
        return self.total

    def add(self, arrived):
        first = (lax.axis_index("dp") // self.step) % 2 == 0
        low = jnp.where(first, self.kept, arrived)
        top = jnp.where(first, arrived, self.kept)
        both = jnp.stack([low, top], axis=1)
        self.total = both.reshape((both.shape[0] * 2,) + both.shape[2:])
        return self.split()

    def launch(self, away):
        if away is not None:
            pairs = [(device, device ^ self.step) for device in range(lax.axis_size("dp"))]
            self.flight = lax.ppermute(away, "dp", pairs)

    def result(self):
        while self.flight is not None:
            self.launch(self.add(self.flight))
        return self.total.reshape((-1, self.total.shape[-1]))


def tick(critical, tasks):
    live = [task for task in tasks if task.flight is not None]
    if not live:
        return critical
    critical, *landed = lax.optimization_barrier((critical, *[task.flight for task in live]))
    away = [task.add(value) for task, value in zip(live, landed)]
    more = [(task, value) for task, value in zip(live, away) if value is not None]
    if more:
        critical, *ready = lax.optimization_barrier((critical, *[value for _, value in more]))
        for (task, _), value in zip(more, ready):
            task.launch(value)
    return critical


def exchange(partial, tasks, sources):
    if lax.axis_size("tensor") != 2:
        return lax.psum(partial, "tensor"), [GradScatter(*pair) for pair in sources]
    arrived = lax.ppermute(partial, "tensor", [(0, 1), (1, 0)])
    live = [task for task in tasks if task.flight is not None]
    operands = [task.flight for task in live] + [array for pair in sources for array in pair]
    partial, *rest = lax.optimization_barrier((partial, *operands))
    for task, value in zip(live, rest):
        task.launch(task.add(value))
    rest = rest[len(live) :]
    made = [GradScatter(rest[at], rest[at + 1]) for at in range(0, len(rest), 2)]
    holders = [task for task in live + made if task.flight is not None]
    arrived, *kept = lax.optimization_barrier((arrived, *[task.kept for task in holders]))
    for task, value in zip(holders, kept):
        task.kept = value
    return partial + arrived, made


def on_device(
    inputs,
    condition,
    cotangent,
    w_qkv,
    b_qv,
    w_out,
    b_out,
    w_up,
    b_up,
    w_down,
    b_down,
    w_mod,
    b_mod,
):
    layers = w_qkv.shape[0]
    batch, seq_len, width = inputs.shape
    local_width = w_qkv.shape[3]
    heads_local = local_width // HEAD_DIM
    mod_cols = w_mod.shape[2]
    score_scale = HEAD_DIM ** (-0.5)
    activated = jax.nn.silu(condition)
    mod_local = (
        jnp.stack([vec_mat(activated, w_mod[index]) for index in range(layers)], axis=0)
        + b_mod[:, None, :]
    )
    mod_whole = pair_gather(mod_local, 2).reshape(layers, batch, 6, width)
    condition_task = RowGather(activated)
    kept = []
    hidden = inputs
    for layer_index in range(layers):
        modulation = mod_whole[layer_index]
        shift_a, scale_a, gate_a = (modulation[:, 0], modulation[:, 1], modulation[:, 2])
        shift_b, scale_b, gate_b = (modulation[:, 3], modulation[:, 4], modulation[:, 5])
        modul_a = layer_norm(hidden) * (1.0 + scale_a[:, None, :]) + shift_a[:, None, :]
        modul_a = lax.optimization_barrier(modul_a)
        projected = jnp.einsum("bsd,dcm->bscm", modul_a, w_qkv[layer_index], precision=high)
        queries = (projected[:, :, 0] + b_qv[layer_index, 0]).reshape(
            batch, seq_len, heads_local, HEAD_DIM
        )
        keys = projected[:, :, 1].reshape(batch, seq_len, heads_local, HEAD_DIM)
        values = (projected[:, :, 2] + b_qv[layer_index, 1]).reshape(
            batch, seq_len, heads_local, HEAD_DIM
        )
        scores = jnp.einsum("bqhe,bkhe->bhqk", queries, keys, precision=high) * score_scale
        log_norm = jax.nn.logsumexp(scores, axis=-1, keepdims=True)
        probs = jnp.exp(scores - log_norm)
        attended = jnp.einsum("bhqk,bkhe->bqhe", probs, values, precision=high).reshape(
            batch, seq_len, local_width
        )
        partial_a = jnp.einsum("bsh,hd->bsd", attended, w_out[layer_index], precision=high)
        attn_branch = pair_sum(partial_a) + b_out[layer_index]
        middle = hidden + gate_a[:, None, :] * attn_branch
        modul_b = layer_norm(middle) * (1.0 + scale_b[:, None, :]) + shift_b[:, None, :]
        modul_b = lax.optimization_barrier(modul_b)
        pre_act = (
            jnp.einsum("bsd,df->bsf", modul_b, w_up[layer_index], precision=high)
            + b_up[layer_index]
        )
        activ = gelu_tanh(pre_act)
        partial_b = jnp.einsum("bsf,fd->bsd", activ, w_down[layer_index], precision=high)
        late = layer_index == layers - 1 and lax.axis_size("tensor") == 2
        if late:
            arriving = lax.ppermute(partial_b, "tensor", [(0, 1), (1, 0)])
            mlp_branch = result = None
        else:
            mlp_branch = pair_sum(partial_b) + b_down[layer_index]
            result = middle + gate_b[:, None, :] * mlp_branch
        kept.append(
            (
                hidden,
                modul_a,
                queries,
                keys,
                values,
                probs,
                attended,
                attn_branch,
                middle,
                modul_b,
                pre_act,
                activ,
                mlp_branch,
            )
        )
        hidden = result
    grad_hidden = cotangent
    silu_grad_part = jnp.zeros((batch, width), jnp.float32)
    matrix_grads = [None] * layers
    pieces = [None] * layers
    older = [condition_task]
    for layer_index in reversed(range(layers)):
        (
            layer_in,
            modul_a,
            queries,
            keys,
            values,
            probs,
            attended,
            attn_branch,
            middle,
            modul_b,
            pre_act,
            activ,
            mlp_branch,
        ) = kept[layer_index]
        modulation = mod_whole[layer_index]
        scale_a, gate_a = (modulation[:, 1], modulation[:, 2])
        scale_b, gate_b = (modulation[:, 4], modulation[:, 5])
        d_branch_b = grad_hidden * gate_b[:, None, :]
        g_b_down = jnp.sum(d_branch_b, axis=(0, 1))
        if layer_index < layers - 1:
            g_w_down = GradScatter(d_branch_b, activ)
        d_activ = jnp.einsum("bsd,fd->bsf", d_branch_b, w_down[layer_index], precision=high)
        d_pre = jax.vjp(gelu_tanh, pre_act)[1](d_activ)[0]
        if layer_index < layers - 1:
            d_pre = tick(d_pre, older + [g_w_down])
        g_b_up = jnp.sum(d_pre, axis=(0, 1))
        partial_d = jnp.einsum("bsf,df->bsd", d_pre, w_up[layer_index], precision=high)
        if layer_index < layers - 1:
            d_modul_b, (g_w_up,) = exchange(partial_d, older, [(modul_b, d_pre)])
        else:
            d_modul_b, (g_w_down, g_w_up) = exchange(
                partial_d, older, [(d_branch_b, activ), (modul_b, d_pre)]
            )
        if mlp_branch is None:
            partial_d, arriving = lax.optimization_barrier((partial_d, arriving))
            mlp_branch = partial_b + arriving + b_down[layer_index]
            hidden = middle + gate_b[:, None, :] * mlp_branch
        d_gate_b = jnp.sum(grad_hidden * mlp_branch, axis=1)
        normed_b, norm_back_b = jax.vjp(layer_norm, middle)
        d_scale_b = jnp.sum(d_modul_b * normed_b, axis=1)
        d_shift_b = jnp.sum(d_modul_b, axis=1)
        d_middle = grad_hidden + norm_back_b(d_modul_b * (1.0 + scale_b[:, None, :]))[0]
        d_branch_a = d_middle * gate_a[:, None, :]
        d_gate_a = jnp.sum(d_middle * attn_branch, axis=1)
        g_b_out = jnp.sum(d_branch_a, axis=(0, 1))
        d_attended = jnp.einsum(
            "bsd,hd->bsh", d_branch_a, w_out[layer_index], precision=high
        ).reshape(batch, seq_len, heads_local, HEAD_DIM)
        d_values = jnp.einsum("bhqk,bqhe->bkhe", probs, d_attended, precision=high)
        d_probs = jnp.einsum("bqhe,bkhe->bhqk", d_attended, values, precision=high)
        attended_heads = attended.reshape(batch, seq_len, heads_local, HEAD_DIM)
        row_dot = jnp.transpose(jnp.sum(d_attended * attended_heads, axis=-1), (0, 2, 1))[..., None]
        d_scores = probs * (d_probs - row_dot) * score_scale
        d_scores = tick(d_scores, older + [g_w_down, g_w_up])
        d_queries = jnp.einsum("bhqk,bkhe->bqhe", d_scores, keys, precision=high)
        d_keys = jnp.einsum("bhqk,bqhe->bkhe", d_scores, queries, precision=high)
        d_proj = jnp.stack([d_queries, d_keys, d_values], axis=2).reshape(
            batch, seq_len, 3, local_width
        )
        d_flat = d_proj.reshape(batch, seq_len, 3 * local_width)
        g_b_qv = jnp.sum(d_flat, axis=(0, 1))
        partial_d = jnp.einsum("bscm,dcm->bsd", d_proj, w_qkv[layer_index], precision=high)
        d_modul_a, (g_w_qkv, g_w_out) = exchange(
            partial_d, older + [g_w_down], [(modul_a, d_flat), (d_branch_a, attended)]
        )
        normed_a, norm_back_a = jax.vjp(layer_norm, layer_in)
        d_scale_a = jnp.sum(d_modul_a * normed_a, axis=1)
        d_shift_a = jnp.sum(d_modul_a, axis=1)
        grad_hidden = d_middle + norm_back_a(d_modul_a * (1.0 + scale_a[:, None, :]))[0]
        d_mod = jnp.stack(
            [d_shift_a, d_scale_a, d_gate_a, d_shift_b, d_scale_b, d_gate_b], axis=1
        ).reshape(batch, 6 * width)
        own_cols = lax.dynamic_slice_in_dim(d_mod, lax.axis_index("tensor") * mod_cols, mod_cols, 1)
        silu_grad_part = silu_grad_part + vec_mat_t(own_cols, w_mod[layer_index])
        matrix_grads[layer_index] = (g_w_qkv, g_w_out, g_w_up, g_w_down)
        biases = (g_b_qv, g_b_out, g_b_up, g_b_down)
        line = jnp.concatenate(biases)[None]
        line = jnp.concatenate([line, jnp.zeros((batch - 1, line.shape[1]), line.dtype)], axis=0)
        rows_task = RowGather(jnp.concatenate([own_cols, line], axis=1))
        pieces[layer_index] = (rows_task, biases)
        older = [g_w_down, g_w_up, g_w_out, g_w_qkv, rows_task]
    block = width // lax.axis_size("dp")
    activated_rows = lax.dynamic_slice_in_dim(
        condition_task.result(), lax.axis_index("dp") * block, block, 1
    )
    mod_grads = [None] * layers
    bias_grads = [None] * layers
    for layer_index in reversed(range(layers)):
        rows_task, biases = pieces[layer_index]
        gathered = rows_task.result()
        mod_grads[layer_index] = jnp.einsum(
            "bd,bm->dm", activated_rows, gathered[:, :mod_cols], precision=high
        )
        sums = jnp.sum(gathered, axis=0)
        found = [sums[:mod_cols]]
        start = mod_cols
        for piece in biases:
            found.append(sums[start : start + piece.shape[0]])
            start += piece.shape[0]
        bias_grads[layer_index] = found
    order = range(layers)
    grad_w_qkv = jnp.stack([matrix_grads[index][0].result() for index in order], axis=0)
    grad_w_out = jnp.stack([matrix_grads[index][1].result().T for index in order], axis=0)
    grad_w_up = jnp.stack([matrix_grads[index][2].result() for index in order], axis=0)
    grad_w_down = jnp.stack([matrix_grads[index][3].result().T for index in order], axis=0)
    grad_b_mod, grad_b_qkv, grad_b_out, grad_b_up, grad_b_down = [
        jnp.stack([bias_grads[index][member] for index in order], axis=0) for member in range(5)
    ]
    grad_b_qv = grad_b_qkv.reshape(layers, 3, local_width)[:, ::2]
    grad_condition = pair_sum(silu_grad_part) * silu_slope(condition)
    return (
        hidden,
        grad_hidden,
        grad_condition,
        grad_w_qkv.reshape(layers, block, 3, local_width),
        grad_b_qv,
        grad_w_out,
        grad_b_out,
        grad_w_up,
        grad_b_up,
        grad_w_down,
        grad_b_down,
        jnp.stack(mod_grads, axis=0),
        grad_b_mod,
    )


def solution(mesh):
    in_specs = (
        P("dp", None, None),
        P("dp", None),
        P("dp", None, None),
        P(None, None, None, "tensor"),
        P(None, None, "tensor"),
        P(None, "tensor", None),
        P(),
        P(None, None, "tensor"),
        P(None, "tensor"),
        P(None, "tensor", None),
        P(),
        P(None, None, "tensor"),
        P(None, "tensor"),
    )
    out_specs = (
        P("dp", None, None),
        P("dp", None, None),
        P("dp", None),
        P(None, "dp", None, "tensor"),
        P(None, None, "tensor"),
        P(None, "tensor", "dp"),
        P(),
        P(None, "dp", "tensor"),
        P(None, "tensor"),
        P(None, "tensor", "dp"),
        P(),
        P(None, "dp", "tensor"),
        P(None, "tensor"),
    )
    return jax.shard_map(
        on_device, mesh=mesh, in_specs=in_specs, out_specs=out_specs, check_vma=False
    )
```
